32 devices in a mesh: groups: 2 (over x), seq: 16 (over z, y, core).
Axes of the slice: x: 2, y: 2, z: 4, core: 2. Of those that a mesh axis runs over, the one named last changes fastest.
Arguments:
- tower_in: bfloat16 [8, 4096, 768], P('groups', 'seq'), parts along dimension 0, may hold values from -6 to 6
- first_norm_scale: float32 [4, 768], replicated, may hold values from 0.5 to 2
- first_norm_shift: float32 [4, 768], replicated, may hold values from -0.5 to 0.5
- conv_weight: bfloat16 [4, 3, 768, 384], replicated, may hold values from -0.125 to 0.125
- mid_scale: float32 [4, 384], replicated, may hold values from 0.5 to 2
- second_norm_shift: float32 [4, 384], replicated, may hold values from -0.5 to 0.5
- point_weight: bfloat16 [4, 384, 768], replicated, may hold values from -0.3125 to 0.3125
Outputs:
- tower_out: bfloat16 [8, 4096, 768], P('groups', 'seq'), parts along dimension 0
The draws below stay inside these ranges and needn't reach their ends.
There are 2 independent parts, one for each index of `groups`. The reference program is written for one: setup_inputs(seed, part) draws one part's arguments, and reference() takes and returns one part's arrays. A program takes and returns all parts, laid end to end along the dimension named above; an argument that names none is the same for every part. Nothing has to cross between parts.
All inputs are finite; a program needn't handle non-finite values.
Results may differ from the reference program's by a relative error of at most 0.017.
Values may be sent and summed in bfloat16 or wider, within the bound.
A program may use at most 64 MiB of HBM per device.

```python
import math
import jax
import jax.numpy as jnp

C = 768
FILTERS = 384
BLOCKS = 4
FIRST_DILATION = 32
TRACKS = 4
NBINS = 4096


def shard_levels(rng, shape, shards, low, high):
    gain, own = 1.0, jax.random.fold_in(rng, 6)
    for position, shards_of in shards:
        draws = jnp.exp(jax.random.uniform(jax.random.fold_in(own, position), (shards_of,), jnp.float32, low / len(shards), high / len(shards)))
        gain = gain * jnp.repeat(draws, shape[position] // shards_of).reshape([-1 if axis == position else 1 for axis in range(len(shape))])
    return gain


def gaussian(stream_key, dims, width, most, shards=(), dtype=jnp.bfloat16):
    loudness = shard_levels(stream_key, dims, shards, -0.22, 0.18) if shards else 1.0
    entries = jax.random.normal(stream_key, dims, jnp.float32) * width * loudness
    return jnp.minimum(jnp.maximum(entries, -most), most).astype(dtype)


def setup_inputs(seed: int = 0, part: int = 0) -> dict:
    key_of = jax.random.split(jax.random.key(seed), 8)
    part_keys = jax.random.split(jax.random.fold_in(key_of[7], part), 8)
    tower_in = gaussian(part_keys[0], (TRACKS, NBINS, C), 1.0, 6.0, ((1, 16),))
    first_norm_scale = jnp.clip(jnp.exp(jax.random.uniform(key_of[1], (BLOCKS, C), jnp.float32, math.log(0.5), math.log(2.0))), 0.5, 2.0)
    first_norm_shift = jnp.clip(jax.random.uniform(key_of[2], (BLOCKS, C), jnp.float32, -0.5, 0.5), -0.5, 0.5)
    conv_weight = gaussian(key_of[3], (BLOCKS, 3, C, FILTERS), (3 * C) ** -0.5, 0.125)
    mid_scale = jnp.clip(jnp.exp(jax.random.uniform(key_of[4], (BLOCKS, FILTERS), jnp.float32, math.log(0.5), math.log(2.0))), 0.5, 2.0)
    second_norm_shift = jnp.clip(jax.random.uniform(key_of[5], (BLOCKS, FILTERS), jnp.float32, -0.5, 0.5), -0.5, 0.5)
    point_weight = gaussian(key_of[6], (BLOCKS, FILTERS, C), FILTERS ** -0.5, 0.3125)
    return {"tower_in": tower_in, "first_norm_scale": first_norm_scale, "first_norm_shift": first_norm_shift, "conv_weight": conv_weight, "mid_scale": mid_scale, "second_norm_shift": second_norm_shift, "point_weight": point_weight}


def normalize(stream, scale_vector, shift_vec):
    return jnp.maximum(stream.astype(jnp.float32) * scale_vector + shift_vec, 0.0)


def reference(tower_in, first_norm_scale, first_norm_shift, conv_weight, mid_scale, second_norm_shift, point_weight):
    stream = tower_in
    tracks, bin_count, channels = stream.shape
    for block_number in range(BLOCKS):
        receptive_span = FIRST_DILATION * 2 ** block_number
        normed = normalize(stream, first_norm_scale[block_number], first_norm_shift[block_number]).astype(jnp.bfloat16)
        padded = jnp.pad(normed, ((0, 0), (receptive_span, receptive_span), (0, 0)))
        summed = jnp.zeros((tracks * bin_count, FILTERS), jnp.float32)
        for kernel_tap_index in range(3):
            window = padded[:, kernel_tap_index * receptive_span:kernel_tap_index * receptive_span + bin_count, :]
            window = window.reshape(tracks * bin_count, channels)
            summed = summed + jnp.dot(window, conv_weight[block_number, kernel_tap_index], preferred_element_type=jnp.float32)
        middle = jnp.maximum(summed * mid_scale[block_number] + second_norm_shift[block_number], 0.0).astype(jnp.bfloat16)
        update = jnp.dot(middle, point_weight[block_number], preferred_element_type=jnp.float32)
        flat = stream.reshape(tracks * bin_count, channels).astype(jnp.float32)
        stream = (flat + update).astype(jnp.bfloat16).reshape(tracks, bin_count, channels)
    return stream
```

```python
import functools

import jax
import jax.numpy as jnp
from jax import lax
from jax.experimental import pallas as pl
from jax.experimental.pallas import tpu as pltpu
from jax.sharding import PartitionSpec as P

FIRST_DILATION = 32
PLANE = 4
MESH = pl.DeviceIdType.MESH


def tower(
    devices,
    blocks,
    stream_hbm,
    first_scale_hbm,
    first_shift_hbm,
    conv_hbm,
    mid_scale_hbm,
    mid_shift_hbm,
    point_hbm,
    out,
    stream,
    conv_w,
    point_w,
    acc,
    first_scale,
    first_shift,
    mid_scale,
    mid_shift,
    norm_sem,
    *rest,
):
    sends = rest[:blocks]
    recvs = rest[blocks : 2 * blocks]
    in_sem, conv_sem, point_sem, send_sem, recv_sem = rest[2 * blocks : 2 * blocks + 5]
    relayed = rest[2 * blocks + 5 :]
    tracks, rows, _ = stream.shape
    filters = acc.shape[2]
    spans = [FIRST_DILATION * 2**b for b in range(blocks)]
    me = lax.axis_index("seq")
    has_left = me > 0
    has_right = me < devices - 1
    left = {"seq": me - 1}
    right = {"seq": me + 1}
    last = blocks - 1

    planes = devices // PLANE
    plane = me // PLANE
    opens = me % PLANE == 0
    closes = me % PLANE == PLANE - 1
    not_first = plane > 0
    not_last = plane < planes - 1
    to_right = lax.div(tracks * (planes - 1 - plane), planes)
    to_left = lax.div(tracks * plane, planes)
    if relayed:
        relay_buf, relay_send, relay_recv = relayed
        via_right = jnp.where(closes & not_last, to_right, 0)
        via_left = jnp.where(opens & not_first, to_left, 0)
        relays = jnp.where(opens & not_last, to_right, 0) + jnp.where(
            closes & not_first, to_left, 0
        )
        mate = {"seq": jnp.where(opens, me + (PLANE - 1), me - (PLANE - 1))}
        target = {"seq": jnp.where(opens, me + PLANE, me - PLANE)}

    def in_copy(t):
        return pltpu.make_async_copy(stream_hbm.at[t], stream.at[t], in_sem.at[t])

    def conv_copy(b, k):
        held = conv_w.at[b, :, pl.ds((0, 2, 1)[k] * filters, filters)]
        return pltpu.make_async_copy(conv_hbm.at[b, k], held, conv_sem.at[b, k])

    def point_copy(b):
        return pltpu.make_async_copy(point_hbm.at[b], point_w.at[b], point_sem.at[b])

    def edge_copy(b, t, side):
        return pltpu.make_async_remote_copy(
            src_ref=sends[b].at[side, t],
            dst_ref=recvs[b].at[side, t],
            send_sem=send_sem.at[b, side, t],
            recv_sem=recv_sem.at[b, side, t],
            device_id=left if side else right,
            device_id_type=MESH,
        )

    def relay_in(t, side):
        return pltpu.make_async_remote_copy(
            src_ref=sends[last].at[side, t],
            dst_ref=relay_buf.at[t],
            send_sem=send_sem.at[last, side, t],
            recv_sem=relay_recv.at[t],
            device_id=mate,
            device_id_type=MESH,
        )

    def relay_out(t, side):
        return pltpu.make_async_remote_copy(
            src_ref=relay_buf.at[t],
            dst_ref=recvs[last].at[side, t],
            send_sem=relay_send.at[t],
            recv_sem=recv_sem.at[last, side, t],
            device_id=target,
            device_id_type=MESH,
        )

    def forward(t, wanted):
        if not relayed:
            return

        @pl.when(wanted & (t < relays))
        def _():
            relay_in(t, 0).wait_recv()

            @pl.when(opens)
            def _():
                relay_out(t, 0).start()

            @pl.when(closes)
            def _():
                relay_out(t, 1).start()

    def send(b, t, side):
        there = has_left if side else has_right
        if relayed and b == last:
            via = t < (via_left if side else via_right)

            @pl.when(via)
            def _():
                relay_in(t, side).start()

            there = there & jnp.logical_not(via)

        @pl.when(there)
        def _():
            edge_copy(b, t, side).start()

    norms = [
        pltpu.make_async_copy(source, held, norm_sem.at[i])
        for i, (source, held) in enumerate(
            (
                (first_scale_hbm, first_scale),
                (first_shift_hbm, first_shift),
                (mid_scale_hbm, mid_scale),
                (mid_shift_hbm, mid_shift),
            )
        )
    ]
    for copy in norms:
        copy.start()
    in_copy(0).start()
    for k in (0, 2, 1):
        conv_copy(0, k).start()
    for t in range(1, tracks):
        in_copy(t).start()
    point_copy(0).start()
    for b in range(1, blocks):
        for k in (0, 2, 1):
            conv_copy(b, k).start()
        point_copy(b).start()

    barrier = pltpu.get_barrier_semaphore()

    @pl.when(has_left)
    def _():
        pl.semaphore_signal(barrier, inc=1, device_id=left, device_id_type=MESH)

    @pl.when(has_right)
    def _():
        pl.semaphore_signal(barrier, inc=1, device_id=right, device_id_type=MESH)

    greeted = has_left.astype(jnp.int32) + has_right.astype(jnp.int32)
    if relayed:
        greeted += jnp.where(
            opens | closes, 1 + not_first.astype(jnp.int32) + not_last.astype(jnp.int32), 0
        )
        for wanted, other in (
            (opens | closes, mate),
            ((opens | closes) & not_first, {"seq": me - PLANE}),
            ((opens | closes) & not_last, {"seq": me + PLANE}),
        ):

            @pl.when(wanted)
            def _():
                pl.semaphore_signal(barrier, inc=1, device_id=other, device_id_type=MESH)

    @pl.when(jnp.logical_not(has_left))
    def _():
        for b in range(blocks):
            recvs[b][0] = jnp.zeros(recvs[b].shape[1:], jnp.bfloat16)

    @pl.when(jnp.logical_not(has_right))
    def _():
        for b in range(blocks):
            recvs[b][1] = jnp.zeros(recvs[b].shape[1:], jnp.bfloat16)

    def first_half(b, t, held, entering=False):
        span = spans[b]
        value = jnp.maximum(
            held.astype(jnp.float32) * first_scale[b : b + 1, :] + first_shift[b : b + 1, :],
            0.0,
        ).astype(jnp.bfloat16)
        taps = jnp.dot(value, conv_w[b], preferred_element_type=jnp.float32)
        low, high = taps[:, :filters], taps[:, filters : 2 * filters]
        centre = taps[:, 2 * filters :]
        sends[b][0, t] = low[rows - span :].astype(jnp.bfloat16)
        sends[b][1, t] = high[:span].astype(jnp.bfloat16)
        if span >= rows:
            acc[t] = centre
        elif 2 * span <= rows:
            acc[t, :span] = centre[:span] + high[span : 2 * span]
            if 2 * span < rows:
                acc[t, span : rows - span] = (
                    centre[span : rows - span] + low[: rows - 2 * span] + high[2 * span :]
                )
            acc[t, rows - span :] = centre[rows - span :] + low[rows - 2 * span : rows - span]
        else:
            acc[t] = centre
            acc[t, span:] += low[: rows - span]
            acc[t, : rows - span] += high[span:]
        if entering:
            pl.semaphore_wait(barrier, greeted)
        send(b, t, 0)
        send(b, t, 1)

    def arrive(b, t):
        @pl.when(has_left)
        def _():
            edge_copy(b, t, 0).wait_recv()

        @pl.when(has_right)
        def _():
            edge_copy(b, t, 1).wait_recv()

    def joined(b, t):
        span = spans[b]
        before = recvs[b][0, t].astype(jnp.float32)
        after = recvs[b][1, t].astype(jnp.float32)
        if span >= rows:
            return acc[t] + before + after
        if 2 * span > rows:
            acc[t, :span] += before
            acc[t, rows - span :] += after
            return acc[t]
        parts = [acc[t, :span] + before]
        if 2 * span < rows:
            parts.append(acc[t, span : rows - span])
        parts.append(acc[t, rows - span :] + after)
        return jnp.concatenate(parts, axis=0)

    def updated(b, held, conv):
        middle = jnp.maximum(
            conv * mid_scale[b : b + 1, :] + mid_shift[b : b + 1, :], 0.0
        ).astype(jnp.bfloat16)
        update = jnp.dot(middle, point_w[b], preferred_element_type=jnp.float32)
        return (held.astype(jnp.float32) + update).astype(jnp.bfloat16)

    def second_half(b, t):
        arrive(b, t)
        held = updated(b, stream[t], joined(b, t))
        stream[t] = held
        return held

    def opening(t, entering=False):
        in_copy(t).wait()
        first_half(0, t, stream[t], entering)

    for copy in norms:
        copy.wait()
    for b in range(blocks):
        for k in (0, 2, 1):
            conv_copy(b, k).wait()
        if b > 0:
            point_copy(b - 1).wait()
        else:
            opening(0, True)

        def step(t, carry, b=b):
            if b == 0:
                opening(t)
            else:
                first_half(b, t, second_half(b - 1, t))
            if b == last:
                forward(t - 2, t >= 2)
            return carry

        lax.fori_loop(0 if b else 1, tracks, step, 0)
    point_copy(last).wait()

    def close(t, carry):
        arrive(last, t)
        out[t] = updated(last, stream[t], joined(last, t))
        forward(tracks - 3 + t, t >= 1)
        return carry

    lax.fori_loop(0, tracks, close, 0)

    def finish(t, carry):
        for b in range(blocks):

            @pl.when(has_right)
            def _():
                edge_copy(b, t, 0).wait_send()

            @pl.when(has_left)
            def _():
                edge_copy(b, t, 1).wait_send()

        if relayed:

            @pl.when(t < relays)
            def _():
                relay_out(t, 0).wait_send()

        return carry

    lax.fori_loop(0, tracks, finish, 0)


def solution(mesh):
    devices = mesh.shape["seq"]

    def local(tower_in, s1, h1, conv, s2, h2, point):
        blocks, taps, channels, filters = conv.shape
        tracks, rows, _ = tower_in.shape
        edges = [
            pltpu.VMEM((2, tracks, FIRST_DILATION * 2**b, filters), jnp.bfloat16)
            for b in range(blocks)
        ]
        relayed = []
        if devices % PLANE == 0 and 1 < devices // PLANE <= tracks and tracks > 2:
            relayed = [
                pltpu.VMEM((tracks, FIRST_DILATION * 2 ** (blocks - 1), filters), jnp.bfloat16),
                pltpu.SemaphoreType.DMA((tracks,)),
                pltpu.SemaphoreType.DMA((tracks,)),
            ]
        vmem = pl.BlockSpec(memory_space=pltpu.VMEM)
        hbm = pl.BlockSpec(memory_space=pltpu.HBM)
        return pl.pallas_call(
            functools.partial(tower, devices, blocks),
            out_shape=pltpu.VMEM(tower_in.shape, tower_in.dtype),
            in_specs=[hbm] * 7,
            out_specs=vmem,
            scratch_shapes=[
                pltpu.VMEM((tracks, rows, channels), jnp.bfloat16),
                pltpu.VMEM((blocks, channels, taps * filters), jnp.bfloat16),
                pltpu.VMEM(point.shape, jnp.bfloat16),
                pltpu.VMEM((tracks, rows, filters), jnp.float32),
                *[pltpu.VMEM(small.shape, jnp.float32) for small in (s1, h1, s2, h2)],
                pltpu.SemaphoreType.DMA((4,)),
                *edges,
                *edges,
                pltpu.SemaphoreType.DMA((tracks,)),
                pltpu.SemaphoreType.DMA((blocks, taps)),
                pltpu.SemaphoreType.DMA((blocks,)),
                pltpu.SemaphoreType.DMA((blocks, 2, tracks)),
                pltpu.SemaphoreType.DMA((blocks, 2, tracks)),
                *relayed,
            ],
            compiler_params=pltpu.CompilerParams(
                collective_id=0,
                has_side_effects=True,
                vmem_limit_bytes=52 * 2**20,
            ),
        )(*[pltpu.with_memory_space_constraint(x, pltpu.HBM) for x in (tower_in, s1, h1, conv, s2, h2, point)])

    placed = (P("groups", "seq", None), P(), P(), P(), P(), P(), P())
    return jax.shard_map(
        local, mesh=mesh, in_specs=placed, out_specs=P("groups", "seq", None), check_vma=False
    )
```

```python
import functools

import jax
import jax.numpy as jnp
from jax import lax
from jax.experimental import pallas as pl
from jax.experimental.pallas import tpu as pltpu
from jax.sharding import PartitionSpec as P

FIRST_DILATION = 32
PLANE = 4
MESH = pl.DeviceIdType.MESH


def tower(
    devices,
    blocks,
    stream_hbm,
    first_scale_hbm,
    first_shift_hbm,
    conv_hbm,
    mid_scale_hbm,
    mid_shift_hbm,
    point_hbm,
    out,
    stream,
    conv_w,
    point_w,
    acc,
    first_scale,
    first_shift,
    mid_scale,
    mid_shift,
    norm_sem,
    *rest,
):
    sends = rest[:blocks]
    recvs = rest[blocks : 2 * blocks]
    in_sem, conv_sem, point_sem, send_sem, recv_sem = rest[2 * blocks : 2 * blocks + 5]
    relayed = rest[2 * blocks + 5 :]
    tracks, rows, _ = stream.shape
    filters = acc.shape[2]
    spans = [FIRST_DILATION * 2**b for b in range(blocks)]
    me = lax.axis_index("seq")
    has_left = me > 0
    has_right = me < devices - 1
    left = {"seq": me - 1}
    right = {"seq": me + 1}
    last = blocks - 1

    planes = devices // PLANE
    plane = me // PLANE
    opens = me % PLANE == 0
    closes = me % PLANE == PLANE - 1
    not_first = plane > 0
    not_last = plane < planes - 1
    to_right = lax.div(tracks * (planes - 1 - plane), planes)
    to_left = lax.div(tracks * plane, planes)
    if relayed:
        relay_buf, relay_send, relay_recv = relayed
        via_right = jnp.where(closes & not_last, to_right, 0)
        via_left = jnp.where(opens & not_first, to_left, 0)
        relays = jnp.where(opens & not_last, to_right, 0) + jnp.where(
            closes & not_first, to_left, 0
        )
        mate = {"seq": jnp.where(opens, me + (PLANE - 1), me - (PLANE - 1))}
        target = {"seq": jnp.where(opens, me + PLANE, me - PLANE)}

    def in_copy(t):
        return pltpu.make_async_copy(stream_hbm.at[t], stream.at[t], in_sem.at[t])

    def conv_copy(b, k):
        held = conv_w.at[b, :, pl.ds((0, 2, 1)[k] * filters, filters)]
        return pltpu.make_async_copy(conv_hbm.at[b, k], held, conv_sem.at[b, k])

    def point_copy(b):
        return pltpu.make_async_copy(point_hbm.at[b], point_w.at[b], point_sem.at[b])

    def edge_copy(b, t, side):
        return pltpu.make_async_remote_copy(
            src_ref=sends[b].at[side, t],
            dst_ref=recvs[b].at[side, t],
            send_sem=send_sem.at[b, side, t],
            recv_sem=recv_sem.at[b, side, t],
            device_id=left if side else right,
            device_id_type=MESH,
        )

    def relay_in(t, side):
        return pltpu.make_async_remote_copy(
            src_ref=sends[last].at[side, t],
            dst_ref=relay_buf.at[t],
            send_sem=send_sem.at[last, side, t],
            recv_sem=relay_recv.at[t],
            device_id=mate,
            device_id_type=MESH,
        )

    def relay_out(t, side):
        return pltpu.make_async_remote_copy(
            src_ref=relay_buf.at[t],
            dst_ref=recvs[last].at[side, t],
            send_sem=relay_send.at[t],
            recv_sem=recv_sem.at[last, side, t],
            device_id=target,
            device_id_type=MESH,
        )

    def forward(t, wanted):
        if not relayed:
            return

        @pl.when(wanted & (t < relays))
        def _():
            relay_in(t, 0).wait_recv()

            @pl.when(opens)
            def _():
                relay_out(t, 0).start()

            @pl.when(closes)
            def _():
                relay_out(t, 1).start()

    def send(b, t, side):
        there = has_left if side else has_right
        if relayed and b == last:
            via = t < (via_left if side else via_right)

            @pl.when(via)
            def _():
                relay_in(t, side).start()

            there = there & jnp.logical_not(via)

        @pl.when(there)
        def _():
            edge_copy(b, t, side).start()

    norms = [
        pltpu.make_async_copy(source, held, norm_sem.at[i])
        for i, (source, held) in enumerate(
            (
                (first_scale_hbm, first_scale),
                (first_shift_hbm, first_shift),
                (mid_scale_hbm, mid_scale),
                (mid_shift_hbm, mid_shift),
            )
        )
    ]
    for copy in norms:
        copy.start()
    in_copy(0).start()
    for k in (0, 2, 1):
        conv_copy(0, k).start()
    for t in range(1, tracks):
        in_copy(t).start()
    point_copy(0).start()
    barrier = pltpu.get_barrier_semaphore()

    @pl.when(has_left)
    def _():
        pl.semaphore_signal(barrier, inc=1, device_id=left, device_id_type=MESH)

    @pl.when(has_right)
    def _():
        pl.semaphore_signal(barrier, inc=1, device_id=right, device_id_type=MESH)

    greeted = has_left.astype(jnp.int32) + has_right.astype(jnp.int32)
    if relayed:
        greeted += jnp.where(
            opens | closes, 1 + not_first.astype(jnp.int32) + not_last.astype(jnp.int32), 0
        )
        for wanted, other in (
            (opens | closes, mate),
            ((opens | closes) & not_first, {"seq": me - PLANE}),
            ((opens | closes) & not_last, {"seq": me + PLANE}),
        ):

            @pl.when(wanted)
            def _():
                pl.semaphore_signal(barrier, inc=1, device_id=other, device_id_type=MESH)

    for b in range(1, blocks):
        for k in (0, 2, 1):
            conv_copy(b, k).start()
        point_copy(b).start()

    @pl.when(jnp.logical_not(has_left))
    def _():
        for b in range(blocks):
            recvs[b][0] = jnp.zeros(recvs[b].shape[1:], jnp.bfloat16)

    @pl.when(jnp.logical_not(has_right))
    def _():
        for b in range(blocks):
            recvs[b][1] = jnp.zeros(recvs[b].shape[1:], jnp.bfloat16)

    def first_half(b, t, held, entering=False):
        span = spans[b]
        value = jnp.maximum(
            held.astype(jnp.float32) * first_scale[b : b + 1, :] + first_shift[b : b + 1, :],
            0.0,
        ).astype(jnp.bfloat16)
        taps = jnp.dot(value, conv_w[b], preferred_element_type=jnp.float32)
        low, high = taps[:, :filters], taps[:, filters : 2 * filters]
        centre = taps[:, 2 * filters :]
        sends[b][0, t] = low[rows - span :].astype(jnp.bfloat16)
        sends[b][1, t] = high[:span].astype(jnp.bfloat16)
        if span >= rows:
            acc[t] = centre
        elif 2 * span <= rows:
            acc[t, :span] = centre[:span] + high[span : 2 * span]
            if 2 * span < rows:
                acc[t, span : rows - span] = (
                    centre[span : rows - span] + low[: rows - 2 * span] + high[2 * span :]
                )
            acc[t, rows - span :] = centre[rows - span :] + low[rows - 2 * span : rows - span]
        else:
            acc[t] = centre
            acc[t, span:] += low[: rows - span]
            acc[t, : rows - span] += high[span:]
        if entering:
            pl.semaphore_wait(barrier, greeted)
        send(b, t, 0)
        send(b, t, 1)

    def arrive(b, t):
        @pl.when(has_left)
        def _():
            edge_copy(b, t, 0).wait_recv()

        @pl.when(has_right)
        def _():
            edge_copy(b, t, 1).wait_recv()

    def joined(b, t):
        span = spans[b]
        before = recvs[b][0, t].astype(jnp.float32)
        after = recvs[b][1, t].astype(jnp.float32)
        if span >= rows:
            return acc[t] + before + after
        if 2 * span > rows:
            acc[t, :span] += before
            acc[t, rows - span :] += after
            return acc[t]
        parts = [acc[t, :span] + before]
        if 2 * span < rows:
            parts.append(acc[t, span : rows - span])
        parts.append(acc[t, rows - span :] + after)
        return jnp.concatenate(parts, axis=0)

    def updated(b, held, conv):
        middle = jnp.maximum(
            conv * mid_scale[b : b + 1, :] + mid_shift[b : b + 1, :], 0.0
        ).astype(jnp.bfloat16)
        update = jnp.dot(middle, point_w[b], preferred_element_type=jnp.float32)
        return (held.astype(jnp.float32) + update).astype(jnp.bfloat16)

    def second_half(b, t):
        arrive(b, t)
        held = updated(b, stream[t], joined(b, t))
        stream[t] = held
        return held

    def opening(t, entering=False):
        in_copy(t).wait()
        first_half(0, t, stream[t], entering)

    for copy in norms:
        copy.wait()
    for b in range(blocks):
        for k in (0, 2, 1):
            conv_copy(b, k).wait()
        if b > 0:
            point_copy(b - 1).wait()
        else:
            opening(0, True)

        def step(t, carry, b=b):
            if b == 0:
                opening(t)
            else:
                first_half(b, t, second_half(b - 1, t))
            if b == last:
                forward(t - 2, t >= 2)
            return carry

        lax.fori_loop(0 if b else 1, tracks, step, 0)
    point_copy(last).wait()

    def close(t, carry):
        arrive(last, t)
        out[t] = updated(last, stream[t], joined(last, t))
        forward(tracks - 3 + t, t >= 1)
        return carry

    lax.fori_loop(0, tracks, close, 0)

    def finish(t, carry):
        for b in range(blocks):

            @pl.when(has_right)
            def _():
                edge_copy(b, t, 0).wait_send()

            @pl.when(has_left)
            def _():
                edge_copy(b, t, 1).wait_send()

        if relayed:

            @pl.when(t < relays)
            def _():
                relay_out(t, 0).wait_send()

        return carry

    lax.fori_loop(0, tracks, finish, 0)


def solution(mesh):
    devices = mesh.shape["seq"]

    def local(tower_in, s1, h1, conv, s2, h2, point):
        blocks, taps, channels, filters = conv.shape
        tracks, rows, _ = tower_in.shape
        edges = [
            pltpu.VMEM((2, tracks, FIRST_DILATION * 2**b, filters), jnp.bfloat16)
            for b in range(blocks)
        ]
        relayed = []
        if devices % PLANE == 0 and 1 < devices // PLANE <= tracks and tracks > 2:
            relayed = [
                pltpu.VMEM((tracks, FIRST_DILATION * 2 ** (blocks - 1), filters), jnp.bfloat16),
                pltpu.SemaphoreType.DMA((tracks,)),
                pltpu.SemaphoreType.DMA((tracks,)),
            ]
        vmem = pl.BlockSpec(memory_space=pltpu.VMEM)
        hbm = pl.BlockSpec(memory_space=pltpu.HBM)
        return pl.pallas_call(
            functools.partial(tower, devices, blocks),
            out_shape=pltpu.VMEM(tower_in.shape, tower_in.dtype),
            in_specs=[hbm] * 7,
            out_specs=vmem,
            scratch_shapes=[
                pltpu.VMEM((tracks, rows, channels), jnp.bfloat16),
                pltpu.VMEM((blocks, channels, taps * filters), jnp.bfloat16),
                pltpu.VMEM(point.shape, jnp.bfloat16),
                pltpu.VMEM((tracks, rows, filters), jnp.float32),
                *[pltpu.VMEM(small.shape, jnp.float32) for small in (s1, h1, s2, h2)],
                pltpu.SemaphoreType.DMA((4,)),
                *edges,
                *edges,
                pltpu.SemaphoreType.DMA((tracks,)),
                pltpu.SemaphoreType.DMA((blocks, taps)),
                pltpu.SemaphoreType.DMA((blocks,)),
                pltpu.SemaphoreType.DMA((blocks, 2, tracks)),
                pltpu.SemaphoreType.DMA((blocks, 2, tracks)),
                *relayed,
            ],
            compiler_params=pltpu.CompilerParams(
                collective_id=0,
                has_side_effects=True,
                vmem_limit_bytes=52 * 2**20,
            ),
        )(*[pltpu.with_memory_space_constraint(x, pltpu.HBM) for x in (tower_in, s1, h1, conv, s2, h2, point)])

    placed = (P("groups", "seq", None), P(), P(), P(), P(), P(), P())
    return jax.shard_map(
        local, mesh=mesh, in_specs=placed, out_specs=P("groups", "seq", None), check_vma=False
    )
```

```python
import functools

import jax
import jax.numpy as jnp
from jax import lax
from jax.experimental import pallas as pl
from jax.experimental.pallas import tpu as pltpu
from jax.sharding import PartitionSpec as P

FIRST_DILATION = 32
PLANE = 4
MESH = pl.DeviceIdType.MESH


def tower(
    devices,
    blocks,
    stream_hbm,
    first_scale_hbm,
    first_shift_hbm,
    conv_hbm,
    mid_scale_hbm,
    mid_shift_hbm,
    point_hbm,
    out,
    stream,
    conv_w,
    point_w,
    acc,
    first_scale,
    first_shift,
    mid_scale,
    mid_shift,
    norm_sem,
    *rest,
):
    sends = rest[:blocks]
    recvs = rest[blocks : 2 * blocks]
    in_sem, conv_sem, point_sem, send_sem, recv_sem = rest[2 * blocks : 2 * blocks + 5]
    relayed = rest[2 * blocks + 5 :]
    tracks, rows, _ = stream.shape
    filters = acc.shape[2]
    spans = [FIRST_DILATION * 2**b for b in range(blocks)]
    me = lax.axis_index("seq")
    has_left = me > 0
    has_right = me < devices - 1
    left = {"seq": me - 1}
    right = {"seq": me + 1}
    last = blocks - 1

    planes = devices // PLANE
    plane = me // PLANE
    opens = me % PLANE == 0
    closes = me % PLANE == PLANE - 1
    not_first = plane > 0
    not_last = plane < planes - 1
    to_right = lax.div(tracks * (planes - 1 - plane), planes)
    to_left = lax.div(tracks * plane, planes)
    if relayed:
        relay_buf, relay_send, relay_recv = relayed
        via_right = jnp.where(closes & not_last, to_right, 0)
        via_left = jnp.where(opens & not_first, to_left, 0)
        relays = jnp.where(opens & not_last, to_right, 0) + jnp.where(
            closes & not_first, to_left, 0
        )
        mate = {"seq": jnp.where(opens, me + (PLANE - 1), me - (PLANE - 1))}
        target = {"seq": jnp.where(opens, me + PLANE, me - PLANE)}

    def in_copy(t):
        return pltpu.make_async_copy(stream_hbm.at[t], stream.at[t], in_sem.at[t])

    def conv_copy(b, k):
        held = conv_w.at[b, :, pl.ds((0, 2, 1)[k] * filters, filters)]
        return pltpu.make_async_copy(conv_hbm.at[b, k], held, conv_sem.at[b, k])

    def point_copy(b):
        return pltpu.make_async_copy(point_hbm.at[b], point_w.at[b], point_sem.at[b])

    def edge_copy(b, t, side):
        return pltpu.make_async_remote_copy(
            src_ref=sends[b].at[side, t],
            dst_ref=recvs[b].at[side, t],
            send_sem=send_sem.at[b, side, t],
            recv_sem=recv_sem.at[b, side, t],
            device_id=left if side else right,
            device_id_type=MESH,
        )

    def relay_in(t, side):
        return pltpu.make_async_remote_copy(
            src_ref=sends[last].at[side, t],
            dst_ref=relay_buf.at[t],
            send_sem=send_sem.at[last, side, t],
            recv_sem=relay_recv.at[t],
            device_id=mate,
            device_id_type=MESH,
        )

    def relay_out(t, side):
        return pltpu.make_async_remote_copy(
            src_ref=relay_buf.at[t],
            dst_ref=recvs[last].at[side, t],
            send_sem=relay_send.at[t],
            recv_sem=recv_sem.at[last, side, t],
            device_id=target,
            device_id_type=MESH,
        )

    def forward(t, wanted):
        if not relayed:
            return

        @pl.when(wanted & (t < relays))
        def _():
            relay_in(t, 0).wait_recv()

            @pl.when(opens)
            def _():
                relay_out(t, 0).start()

            @pl.when(closes)
            def _():
                relay_out(t, 1).start()

    def send(b, t, side):
        there = has_left if side else has_right
        if relayed and b == last:
            via = t < (via_left if side else via_right)

            @pl.when(via)
            def _():
                relay_in(t, side).start()

            there = there & jnp.logical_not(via)

        @pl.when(there)
        def _():
            edge_copy(b, t, side).start()

    norms = [
        pltpu.make_async_copy(source, held, norm_sem.at[i])
        for i, (source, held) in enumerate(
            (
                (first_scale_hbm, first_scale),
                (first_shift_hbm, first_shift),
                (mid_scale_hbm, mid_scale),
                (mid_shift_hbm, mid_shift),
            )
        )
    ]
    for copy in norms:
        copy.start()
    in_copy(0).start()
    for k in (0, 2, 1):
        conv_copy(0, k).start()
    for t in range(1, tracks):
        in_copy(t).start()
    point_copy(0).start()
    barrier = pltpu.get_barrier_semaphore()

    @pl.when(has_left)
    def _():
        pl.semaphore_signal(barrier, inc=1, device_id=left, device_id_type=MESH)

    @pl.when(has_right)
    def _():
        pl.semaphore_signal(barrier, inc=1, device_id=right, device_id_type=MESH)

    greeted = has_left.astype(jnp.int32) + has_right.astype(jnp.int32)
    if relayed:
        greeted += jnp.where(
            opens | closes, 1 + not_first.astype(jnp.int32) + not_last.astype(jnp.int32), 0
        )
        for wanted, other in (
            (opens | closes, mate),
            ((opens | closes) & not_first, {"seq": me - PLANE}),
            ((opens | closes) & not_last, {"seq": me + PLANE}),
        ):

            @pl.when(wanted)
            def _():
                pl.semaphore_signal(barrier, inc=1, device_id=other, device_id_type=MESH)

    for b in range(1, blocks):
        for k in (0, 2, 1):
            conv_copy(b, k).start()
        point_copy(b).start()

    @pl.when(jnp.logical_not(has_left))
    def _():
        for b in range(blocks):
            recvs[b][0] = jnp.zeros(recvs[b].shape[1:], jnp.bfloat16)

    @pl.when(jnp.logical_not(has_right))
    def _():
        for b in range(blocks):
            recvs[b][1] = jnp.zeros(recvs[b].shape[1:], jnp.bfloat16)

    def first_half(b, t, held, entering=False):
        span = spans[b]
        value = jnp.maximum(
            held.astype(jnp.float32) * first_scale[b : b + 1, :] + first_shift[b : b + 1, :],
            0.0,
        ).astype(jnp.bfloat16)
        if entering:
            outer = jnp.dot(
                value, conv_w[b, :, : 2 * filters], preferred_element_type=jnp.float32
            )
            low, high = outer[:, :filters], outer[:, filters:]
            sends[b][0, t] = low[rows - span :].astype(jnp.bfloat16)
            sends[b][1, t] = high[:span].astype(jnp.bfloat16)
            pl.semaphore_wait(barrier, greeted)
            send(b, t, 0)
            send(b, t, 1)
            conv_copy(b, 1).wait()
            centre = jnp.dot(value, conv_w[b, :, 2 * filters :], preferred_element_type=jnp.float32)
        else:
            taps = jnp.dot(value, conv_w[b], preferred_element_type=jnp.float32)
            low, high = taps[:, :filters], taps[:, filters : 2 * filters]
            centre = taps[:, 2 * filters :]
            sends[b][0, t] = low[rows - span :].astype(jnp.bfloat16)
            sends[b][1, t] = high[:span].astype(jnp.bfloat16)
        if span >= rows:
            acc[t] = centre
        elif 2 * span <= rows:
            acc[t, :span] = centre[:span] + high[span : 2 * span]
            if 2 * span < rows:
                acc[t, span : rows - span] = (
                    centre[span : rows - span] + low[: rows - 2 * span] + high[2 * span :]
                )
            acc[t, rows - span :] = centre[rows - span :] + low[rows - 2 * span : rows - span]
        else:
            acc[t] = centre
            acc[t, span:] += low[: rows - span]
            acc[t, : rows - span] += high[span:]
        if not entering:
            send(b, t, 0)
            send(b, t, 1)

    def arrive(b, t):
        @pl.when(has_left)
        def _():
            edge_copy(b, t, 0).wait_recv()

        @pl.when(has_right)
        def _():
            edge_copy(b, t, 1).wait_recv()

    def joined(b, t):
        span = spans[b]
        before = recvs[b][0, t].astype(jnp.float32)
        after = recvs[b][1, t].astype(jnp.float32)
        if span >= rows:
            return acc[t] + before + after
        if 2 * span > rows:
            acc[t, :span] += before
            acc[t, rows - span :] += after
            return acc[t]
        parts = [acc[t, :span] + before]
        if 2 * span < rows:
            parts.append(acc[t, span : rows - span])
        parts.append(acc[t, rows - span :] + after)
        return jnp.concatenate(parts, axis=0)

    def updated(b, held, conv):
        middle = jnp.maximum(
            conv * mid_scale[b : b + 1, :] + mid_shift[b : b + 1, :], 0.0
        ).astype(jnp.bfloat16)
        update = jnp.dot(middle, point_w[b], preferred_element_type=jnp.float32)
        return (held.astype(jnp.float32) + update).astype(jnp.bfloat16)

    def second_half(b, t):
        arrive(b, t)
        held = updated(b, stream[t], joined(b, t))
        stream[t] = held
        return held

    def opening(t, entering=False):
        in_copy(t).wait()
        first_half(0, t, stream[t], entering)

    for copy in norms:
        copy.wait()
    for b in range(blocks):
        for k in (0, 2, 1) if b else (0, 2):
            conv_copy(b, k).wait()
        if b > 0:
            point_copy(b - 1).wait()
        else:
            opening(0, True)

        def step(t, carry, b=b):
            if b == 0:
                opening(t)
            else:
                first_half(b, t, second_half(b - 1, t))
            if b == last:
                forward(t - 2, t >= 2)
            return carry

        lax.fori_loop(0 if b else 1, tracks, step, 0)
    point_copy(last).wait()

    def close(t, carry):
        arrive(last, t)
        out[t] = updated(last, stream[t], joined(last, t))
        forward(tracks - 3 + t, t >= 1)
        return carry

    lax.fori_loop(0, tracks, close, 0)

    def finish(t, carry):
        for b in range(blocks):

            @pl.when(has_right)
            def _():
                edge_copy(b, t, 0).wait_send()

            @pl.when(has_left)
            def _():
                edge_copy(b, t, 1).wait_send()

        if relayed:

            @pl.when(t < relays)
            def _():
                relay_out(t, 0).wait_send()

        return carry

    lax.fori_loop(0, tracks, finish, 0)


def solution(mesh):
    devices = mesh.shape["seq"]

    def local(tower_in, s1, h1, conv, s2, h2, point):
        blocks, taps, channels, filters = conv.shape
        tracks, rows, _ = tower_in.shape
        edges = [
            pltpu.VMEM((2, tracks, FIRST_DILATION * 2**b, filters), jnp.bfloat16)
            for b in range(blocks)
        ]
        relayed = []
        if devices % PLANE == 0 and 1 < devices // PLANE <= tracks and tracks > 2:
            relayed = [
                pltpu.VMEM((tracks, FIRST_DILATION * 2 ** (blocks - 1), filters), jnp.bfloat16),
                pltpu.SemaphoreType.DMA((tracks,)),
                pltpu.SemaphoreType.DMA((tracks,)),
            ]
        vmem = pl.BlockSpec(memory_space=pltpu.VMEM)
        hbm = pl.BlockSpec(memory_space=pltpu.HBM)
        return pl.pallas_call(
            functools.partial(tower, devices, blocks),
            out_shape=pltpu.VMEM(tower_in.shape, tower_in.dtype),
            in_specs=[hbm] * 7,
            out_specs=vmem,
            scratch_shapes=[
                pltpu.VMEM((tracks, rows, channels), jnp.bfloat16),
                pltpu.VMEM((blocks, channels, taps * filters), jnp.bfloat16),
                pltpu.VMEM(point.shape, jnp.bfloat16),
                pltpu.VMEM((tracks, rows, filters), jnp.float32),
                *[pltpu.VMEM(small.shape, jnp.float32) for small in (s1, h1, s2, h2)],
                pltpu.SemaphoreType.DMA((4,)),
                *edges,
                *edges,
                pltpu.SemaphoreType.DMA((tracks,)),
                pltpu.SemaphoreType.DMA((blocks, taps)),
                pltpu.SemaphoreType.DMA((blocks,)),
                pltpu.SemaphoreType.DMA((blocks, 2, tracks)),
                pltpu.SemaphoreType.DMA((blocks, 2, tracks)),
                *relayed,
            ],
            compiler_params=pltpu.CompilerParams(
                collective_id=0,
                has_side_effects=True,
                vmem_limit_bytes=52 * 2**20,
            ),
        )(*[pltpu.with_memory_space_constraint(x, pltpu.HBM) for x in (tower_in, s1, h1, conv, s2, h2, point)])

    placed = (P("groups", "seq", None), P(), P(), P(), P(), P(), P())
    return jax.shard_map(
        local, mesh=mesh, in_specs=placed, out_specs=P("groups", "seq", None), check_vma=False
    )
```

```python
import functools

import jax
import jax.numpy as jnp
from jax import lax
from jax.experimental import pallas as pl
from jax.experimental.pallas import tpu as pltpu
from jax.sharding import PartitionSpec as P

FIRST_DILATION = 32
PLANE = 4
MESH = pl.DeviceIdType.MESH


def tower(
    devices,
    blocks,
    stream_hbm,
    first_scale_hbm,
    first_shift_hbm,
    conv_hbm,
    mid_scale_hbm,
    mid_shift_hbm,
    point_hbm,
    out,
    stream,
    conv_w,
    point_w,
    acc,
    first_scale,
    first_shift,
    mid_scale,
    mid_shift,
    norm_sem,
    *rest,
):
    sends = rest[:blocks]
    recvs = rest[blocks : 2 * blocks]
    in_sem, conv_sem, point_sem, send_sem, recv_sem = rest[2 * blocks : 2 * blocks + 5]
    relayed = rest[2 * blocks + 5 :]
    tracks, rows, _ = stream.shape
    filters = acc.shape[2]
    spans = [FIRST_DILATION * 2**b for b in range(blocks)]
    me = lax.axis_index("seq")
    has_left = me > 0
    has_right = me < devices - 1
    left = {"seq": me - 1}
    right = {"seq": me + 1}
    last = blocks - 1

    planes = devices // PLANE
    plane = me // PLANE
    opens = me % PLANE == 0
    closes = me % PLANE == PLANE - 1
    not_first = plane > 0
    not_last = plane < planes - 1
    to_right = lax.div(tracks * (planes - 1 - plane), planes)
    to_left = lax.div(tracks * plane, planes)
    if relayed:
        relay_buf, relay_send, relay_recv = relayed
        via_right = jnp.where(closes & not_last, to_right, 0)
        via_left = jnp.where(opens & not_first, to_left, 0)
        relays = jnp.where(opens & not_last, to_right, 0) + jnp.where(
            closes & not_first, to_left, 0
        )
        mate = {"seq": jnp.where(opens, me + (PLANE - 1), me - (PLANE - 1))}
        target = {"seq": jnp.where(opens, me + PLANE, me - PLANE)}

    def in_copy(t):
        return pltpu.make_async_copy(stream_hbm.at[t], stream.at[t], in_sem.at[t])

    def conv_copy(b, k):
        held = conv_w.at[b, :, pl.ds((0, 2, 1)[k] * filters, filters)]
        return pltpu.make_async_copy(conv_hbm.at[b, k], held, conv_sem.at[b, k])

    def point_copy(b):
        return pltpu.make_async_copy(point_hbm.at[b], point_w.at[b], point_sem.at[b])

    def edge_copy(b, t, side):
        return pltpu.make_async_remote_copy(
            src_ref=sends[b].at[side, t],
            dst_ref=recvs[b].at[side, t],
            send_sem=send_sem.at[b, side, t],
            recv_sem=recv_sem.at[b, side, t],
            device_id=left if side else right,
            device_id_type=MESH,
        )

    def relay_in(t, side):
        return pltpu.make_async_remote_copy(
            src_ref=sends[last].at[side, t],
            dst_ref=relay_buf.at[t],
            send_sem=send_sem.at[last, side, t],
            recv_sem=relay_recv.at[t],
            device_id=mate,
            device_id_type=MESH,
        )

    def relay_out(t, side):
        return pltpu.make_async_remote_copy(
            src_ref=relay_buf.at[t],
            dst_ref=recvs[last].at[side, t],
            send_sem=relay_send.at[t],
            recv_sem=recv_sem.at[last, side, t],
            device_id=target,
            device_id_type=MESH,
        )

    def forward(t, wanted):
        if not relayed:
            return

        @pl.when(wanted & (t < relays))
        def _():
            relay_in(t, 0).wait_recv()

            @pl.when(opens)
            def _():
                relay_out(t, 0).start()

            @pl.when(closes)
            def _():
                relay_out(t, 1).start()

    def send(b, t, side):
        there = has_left if side else has_right
        if relayed and b == last:
            via = t < (via_left if side else via_right)

            @pl.when(via)
            def _():
                relay_in(t, side).start()

            there = there & jnp.logical_not(via)

        @pl.when(there)
        def _():
            edge_copy(b, t, side).start()

    norms = [
        pltpu.make_async_copy(source, held, norm_sem.at[i])
        for i, (source, held) in enumerate(
            (
                (first_scale_hbm, first_scale),
                (first_shift_hbm, first_shift),
                (mid_scale_hbm, mid_scale),
                (mid_shift_hbm, mid_shift),
            )
        )
    ]
    for copy in norms:
        copy.start()
    in_copy(0).start()
    for k in (0, 2, 1):
        conv_copy(0, k).start()
    for t in range(1, tracks):
        in_copy(t).start()
    point_copy(0).start()
    barrier = pltpu.get_barrier_semaphore()

    @pl.when(has_left)
    def _():
        pl.semaphore_signal(barrier, inc=1, device_id=left, device_id_type=MESH)

    @pl.when(has_right)
    def _():
        pl.semaphore_signal(barrier, inc=1, device_id=right, device_id_type=MESH)

    greeted = has_left.astype(jnp.int32) + has_right.astype(jnp.int32)
    if relayed:
        greeted += jnp.where(
            opens | closes, 1 + not_first.astype(jnp.int32) + not_last.astype(jnp.int32), 0
        )
        for wanted, other in (
            (opens | closes, mate),
            ((opens | closes) & not_first, {"seq": me - PLANE}),
            ((opens | closes) & not_last, {"seq": me + PLANE}),
        ):

            @pl.when(wanted)
            def _():
                pl.semaphore_signal(barrier, inc=1, device_id=other, device_id_type=MESH)

    for b in range(1, blocks):
        for k in (0, 2, 1):
            conv_copy(b, k).start()
        point_copy(b).start()

    @pl.when(jnp.logical_not(has_left))
    def _():
        for b in range(blocks):
            recvs[b][0] = jnp.zeros(recvs[b].shape[1:], jnp.bfloat16)

    @pl.when(jnp.logical_not(has_right))
    def _():
        for b in range(blocks):
            recvs[b][1] = jnp.zeros(recvs[b].shape[1:], jnp.bfloat16)

    def first_half(b, t, held, entering=False):
        span = spans[b]
        value = jnp.maximum(
            held.astype(jnp.float32) * first_scale[b : b + 1, :] + first_shift[b : b + 1, :],
            0.0,
        ).astype(jnp.bfloat16)
        if entering:
            outer = jnp.dot(
                value, conv_w[b, :, : 2 * filters], preferred_element_type=jnp.float32
            )
            low, high = outer[:, :filters], outer[:, filters:]
            sends[b][0, t] = low[rows - span :].astype(jnp.bfloat16)
            sends[b][1, t] = high[:span].astype(jnp.bfloat16)
            pl.semaphore_wait(barrier, greeted)
            send(b, t, 0)
            send(b, t, 1)
            conv_copy(b, 1).wait()
            centre = jnp.dot(value, conv_w[b, :, 2 * filters :], preferred_element_type=jnp.float32)
        else:
            taps = jnp.dot(value, conv_w[b], preferred_element_type=jnp.float32)
            low, high = taps[:, :filters], taps[:, filters : 2 * filters]
            centre = taps[:, 2 * filters :]
            sends[b][0, t] = low[rows - span :].astype(jnp.bfloat16)
            sends[b][1, t] = high[:span].astype(jnp.bfloat16)
        if span >= rows:
            acc[t] = centre
        elif 2 * span <= rows:
            acc[t, :span] = centre[:span] + high[span : 2 * span]
            if 2 * span < rows:
                acc[t, span : rows - span] = (
                    centre[span : rows - span] + low[: rows - 2 * span] + high[2 * span :]
                )
            acc[t, rows - span :] = centre[rows - span :] + low[rows - 2 * span : rows - span]
        else:
            acc[t] = centre
            acc[t, span:] += low[: rows - span]
            acc[t, : rows - span] += high[span:]
        if not entering:
            send(b, t, 0)
            send(b, t, 1)

    def arrive(b, t):
        @pl.when(has_left)
        def _():
            edge_copy(b, t, 0).wait_recv()

        @pl.when(has_right)
        def _():
            edge_copy(b, t, 1).wait_recv()

    def joined(b, t):
        span = spans[b]
        before = recvs[b][0, t].astype(jnp.float32)
        after = recvs[b][1, t].astype(jnp.float32)
        if span >= rows:
            return acc[t] + before + after
        if 2 * span > rows:
            acc[t, :span] += before
            acc[t, rows - span :] += after
            return acc[t]
        parts = [acc[t, :span] + before]
        if 2 * span < rows:
            parts.append(acc[t, span : rows - span])
        parts.append(acc[t, rows - span :] + after)
        return jnp.concatenate(parts, axis=0)

    def updated(b, held, conv):
        middle = jnp.maximum(
            conv * mid_scale[b : b + 1, :] + mid_shift[b : b + 1, :], 0.0
        ).astype(jnp.bfloat16)
        update = jnp.dot(middle, point_w[b], preferred_element_type=jnp.float32)
        return (held.astype(jnp.float32) + update).astype(jnp.bfloat16)

    def second_half(b, t):
        arrive(b, t)
        held = updated(b, stream[t], joined(b, t))
        stream[t] = held
        return held

    def opening(t, entering=False):
        in_copy(t).wait()
        first_half(0, t, stream[t], entering)

    for copy in norms:
        copy.wait()
    for b in range(blocks):
        for k in (0, 2, 1) if b else (0, 2):
            conv_copy(b, k).wait()
        if b > 0:
            point_copy(b - 1).wait()
        else:
            opening(0, True)

        def step(t, carry, b=b):
            if b == 0:
                opening(t)
            else:
                first_half(b, t, second_half(b - 1, t))
            if b == last:
                forward(t - 2, t >= 2)
            return carry

        lax.fori_loop(0 if b else 1, tracks, step, 0)
    point_copy(last).wait()

    def close(t, carry):
        forward(tracks - 3 + t, t >= 1)
        arrive(last, t)
        out[t] = updated(last, stream[t], joined(last, t))
        return carry

    lax.fori_loop(0, tracks, close, 0)

    def finish(t, carry):
        for b in range(blocks):

            @pl.when(has_right)
            def _():
                edge_copy(b, t, 0).wait_send()

            @pl.when(has_left)
            def _():
                edge_copy(b, t, 1).wait_send()

        if relayed:

            @pl.when(t < relays)
            def _():
                relay_out(t, 0).wait_send()

        return carry

    lax.fori_loop(0, tracks, finish, 0)


def solution(mesh):
    devices = mesh.shape["seq"]

    def local(tower_in, s1, h1, conv, s2, h2, point):
        blocks, taps, channels, filters = conv.shape
        tracks, rows, _ = tower_in.shape
        edges = [
            pltpu.VMEM((2, tracks, FIRST_DILATION * 2**b, filters), jnp.bfloat16)
            for b in range(blocks)
        ]
        relayed = []
        if devices % PLANE == 0 and 1 < devices // PLANE <= tracks and tracks > 2:
            relayed = [
                pltpu.VMEM((tracks, FIRST_DILATION * 2 ** (blocks - 1), filters), jnp.bfloat16),
                pltpu.SemaphoreType.DMA((tracks,)),
                pltpu.SemaphoreType.DMA((tracks,)),
            ]
        vmem = pl.BlockSpec(memory_space=pltpu.VMEM)
        hbm = pl.BlockSpec(memory_space=pltpu.HBM)
        return pl.pallas_call(
            functools.partial(tower, devices, blocks),
            out_shape=pltpu.VMEM(tower_in.shape, tower_in.dtype),
            in_specs=[hbm] * 7,
            out_specs=vmem,
            scratch_shapes=[
                pltpu.VMEM((tracks, rows, channels), jnp.bfloat16),
                pltpu.VMEM((blocks, channels, taps * filters), jnp.bfloat16),
                pltpu.VMEM(point.shape, jnp.bfloat16),
                pltpu.VMEM((tracks, rows, filters), jnp.float32),
                *[pltpu.VMEM(small.shape, jnp.float32) for small in (s1, h1, s2, h2)],
                pltpu.SemaphoreType.DMA((4,)),
                *edges,
                *edges,
                pltpu.SemaphoreType.DMA((tracks,)),
                pltpu.SemaphoreType.DMA((blocks, taps)),
                pltpu.SemaphoreType.DMA((blocks,)),
                pltpu.SemaphoreType.DMA((blocks, 2, tracks)),
                pltpu.SemaphoreType.DMA((blocks, 2, tracks)),
                *relayed,
            ],
            compiler_params=pltpu.CompilerParams(
                collective_id=0,
                has_side_effects=True,
                vmem_limit_bytes=52 * 2**20,
            ),
        )(*[pltpu.with_memory_space_constraint(x, pltpu.HBM) for x in (tower_in, s1, h1, conv, s2, h2, point)])

    placed = (P("groups", "seq", None), P(), P(), P(), P(), P(), P())
    return jax.shard_map(
        local, mesh=mesh, in_specs=placed, out_specs=P("groups", "seq", None), check_vma=False
    )
```
